32 devices in a mesh: hid: 4 (over y, x), tok: 8 (over z, core).
Axes of the slice: x: 2, y: 2, z: 4, core: 2. Of those that a mesh axis runs over, the one named last changes fastest.
Arguments:
- keys: bfloat16 [2, 512, 1280], P(None, 'tok'), may hold values from -6 to 6
- values: bfloat16 [2, 512, 1280], P(None, 'tok'), may hold values from -6 to 6
- queries: bfloat16 [512, 1280], P('tok'), may hold values from -6 to 6
- rates: float32 [2, 512], P(None, 'tok'), may hold values from 0.01 to 0.1
- forget: float32 [2], replicated, may hold values from 0.05 to 0.3
- momentum: float32 [1], replicated, may hold values from 0.5 to 0.95
- write_weight: float32 [1280, 1280], P('tok', 'hid'), may hold values from -0.15625 to 0.15625
- read_weight: float32 [1280, 1280], P('tok', 'hid'), may hold values from -0.15625 to 0.15625
Outputs:
- new_write: float32 [1280, 1280], P('tok', 'hid')
- new_read: float32 [1280, 1280], P('tok', 'hid')
- recalled: bfloat16 [512, 1280], P('tok')
The draws below stay inside these ranges and needn't reach their ends.
All inputs are finite; a program needn't handle non-finite values.
Results may differ from the reference program's by a relative error of at most 0.003.
Values may be sent and summed in bfloat16 or wider, within the bound.
No kernel may reach another device: no remote copies, remote signals or barrier semaphores. Data moves between devices by JAX's collectives and lax.ppermute only.
A program may use at most 64 MiB of HBM per device.

```python
import math
import jax
import jax.numpy as jnp
from jax import lax

D = 1280
H = 1280
TOKENS = 512


def shard_levels(key, dims, pieces, least, top_value):
    def one(axis_at, blocks):
        heights = jax.random.uniform(jax.random.fold_in(jax.random.fold_in(key, 6), axis_at), (blocks,), jnp.float32, least / len(pieces), top_value / len(pieces))
        return jnp.repeat(jnp.exp(heights), dims[axis_at] // blocks).reshape((-1,) + (1,) * (len(dims) - axis_at - 1))

    factor_of = one(*pieces[0])
    for cut in pieces[1:]:
        factor_of = factor_of * one(*cut)
    return factor_of


def gaussian(rng, dims, scale, reach, pieces=(), kind=jnp.bfloat16):
    loudness = shard_levels(rng, dims, pieces, -0.22, 0.18) if pieces else 1.0
    drawn = jax.random.normal(rng, dims, jnp.float32) * scale * loudness
    return jnp.minimum(jnp.maximum(drawn, -reach), reach).astype(kind)


def setup_inputs(seed: int = 0) -> dict:
    key_of = jax.random.split(jax.random.key(seed), 9)
    return {
        "keys": gaussian(key_of[0], (2, TOKENS, D), 1.0, 6.0, ((1, 8),)),
        "values": gaussian(key_of[1], (2, TOKENS, D), 1.0, 6.0, ((1, 8),)),
        "queries": gaussian(key_of[2], (TOKENS, D), 1.0, 6.0, ((0, 8),)),
        "rates": jnp.clip(jnp.exp(math.log(0.1) - 2.3025851 * jax.random.uniform(key_of[3], (2, TOKENS), jnp.float32) ** shard_levels(key_of[3], (2, TOKENS), ((1, 8),), -0.2, 0.2)), 0.01, 0.1),
        "forget": jnp.clip(jax.random.uniform(key_of[4], (2,), jnp.float32, 0.05, 0.3), 0.05, 0.3),
        "momentum": jnp.clip(jax.random.uniform(key_of[5], (1,), jnp.float32, 0.5, 0.95), 0.5, 0.95),
        "write_weight": gaussian(key_of[6], (D, H), D ** -0.5, 0.15625, ((0, 8), (1, 4)), jnp.float32),
        "read_weight": gaussian(key_of[7], (D, H), H ** -0.5, 0.15625, ((0, 8), (1, 4)), jnp.float32),
    }


highest = lax.Precision.HIGHEST
radius = 12.0

def silu_slope(z):
    sig = jax.nn.sigmoid(z)
    return sig * (1.0 + z * (1.0 - sig))

def block_grads(keys_one, values_one, rate_one, write_weight, read_weight):
    inputs = keys_one.astype(jnp.float32)
    hidden_pre = jnp.dot(inputs, write_weight, precision=highest)
    hidden = jax.nn.silu(hidden_pre)
    output = jnp.dot(hidden, read_weight.T, precision=highest)
    error = inputs + output - values_one.astype(jnp.float32)
    delta = 2.0 * rate_one[:, None] * error
    back = jnp.dot(delta, read_weight, precision=highest) * silu_slope(hidden_pre)
    grad_write = jnp.dot(inputs.T, back, precision=highest)
    grad_read = jnp.dot(delta.T, hidden, precision=highest)
    return (grad_write, grad_read)

def reference(keys, values, queries, rates, forget, momentum, write_weight, read_weight):
    first_w, first_r = block_grads(keys[0], values[0], rates[0], write_weight, read_weight)
    second_w, second_r = block_grads(keys[1], values[1], rates[1], write_weight, read_weight)
    factor = 1.0 - forget[1] + momentum[0]
    update_w = factor * first_w + second_w
    update_r = factor * first_r + second_r
    total = jnp.sum(update_w * update_w) + jnp.sum(update_r * update_r)
    scale = jnp.minimum(1.0, radius / jnp.sqrt(total + 1e-06))
    keep = (1.0 - forget[0]) * (1.0 - forget[1])
    new_write = keep * write_weight - scale * update_w
    new_read = keep * read_weight - scale * update_r
    asked = queries.astype(jnp.float32)
    hidden = jax.nn.silu(jnp.dot(asked, new_write, precision=highest))
    recalled = asked + jnp.dot(hidden, new_read.T, precision=highest)
    return (new_write, new_read, recalled.astype(jnp.bfloat16))
```

```python
import jax
import jax.numpy as jnp
from jax import lax
from jax.sharding import PartitionSpec as P

highest = lax.Precision.HIGHEST
radius = 12.0
wire = jnp.bfloat16


def silu_slope(z):
    sig = jax.nn.sigmoid(z)
    return sig * (1.0 + z * (1.0 - sig))


def contract(left, right, left_dim, right_dim):
    return lax.dot_general(
        left,
        right,
        (((left_dim,), (right_dim,)), ((), ())),
        preferred_element_type=jnp.float32,
    )


def regroup(x, hid):
    parts = x.reshape((2, 2, x.shape[0] // 4) + x.shape[1:])
    parts = jnp.where(hid % 2 == 1, parts[:, ::-1], parts)
    parts = jnp.where(hid // 2 == 1, parts[::-1], parts)
    return parts.reshape(x.shape)


def few_devices(keys, values, queries, rates, forget, momentum, write_weight, read_weight):
    width = keys.shape[2]
    tok_count = lax.axis_size("tok")
    chips = tok_count // 2
    hid, tok = lax.axis_index("hid"), lax.axis_index("tok")
    chip, core = tok // 2, tok % 2
    rows, cols = write_weight.shape
    half = cols // 2
    strip = 2 * rows

    def other_core(x):
        return lax.ppermute(x, "tok", [(i, i ^ 1) for i in range(tok_count)])

    def from_chip(x, step):
        pairs = [((i + 2 * step) % tok_count, i) for i in range(tok_count)]
        return lax.ppermute(x, "tok", pairs)

    def to_chip(x, step):
        pairs = [(i, (i + 2 * step) % tok_count) for i in range(tok_count)]
        return lax.ppermute(x, "tok", pairs)

    def with_peer(x, k):
        return lax.ppermute(x, "hid", [(i, i ^ k) for i in range(4)])

    def by_features(x):
        turned = jnp.stack([x[:, strip * j : strip * (j + 1)] for j in range(chips)])
        turned = jnp.concatenate([turned, turned], axis=0)
        turned = lax.dynamic_slice_in_dim(turned, chip, chips, axis=0)
        got = [turned[0]] + [from_chip(turned[(chips - s) % chips], s) for s in range(1, chips)]
        mine = jnp.stack(got)
        groups = jnp.stack([mine] + [with_peer(mine, k) for k in range(1, 4)], axis=1)
        both = jnp.stack([groups, other_core(groups)], axis=1)
        return both

    key_rows = regroup(keys.reshape(-1, width), hid)
    value_rows = regroup(values.reshape(-1, width), hid)
    query_rows = regroup(queries, hid)
    factor = 1.0 - forget[1] + momentum[0]
    per_block = jnp.stack([factor, jnp.ones_like(factor)])
    row_scale = regroup((2.0 * rates * per_block[:, None]).reshape(-1, 1), hid)
    tokens, asked_count = key_rows.shape[0], query_rows.shape[0]

    packed = jnp.concatenate([write_weight.astype(wire), read_weight.astype(wire)], axis=1)
    mine = jnp.stack([packed] + [from_chip(packed, s) for s in range(1, chips)])

    everything = other_core(jnp.concatenate([key_rows, value_rows, query_rows], axis=0))
    key_pair = jnp.concatenate([key_rows, everything[:tokens]], axis=0)
    value_pair = jnp.concatenate([value_rows, everything[tokens : 2 * tokens]], axis=0)
    query_pair = jnp.concatenate([query_rows, everything[2 * tokens :]], axis=0)
    scale_pair = jnp.concatenate([row_scale, other_core(row_scale.reshape(1, -1)).reshape(-1, 1)])

    halves = mine.reshape(chips, rows, 2, 2, half)
    keep_half = jnp.where(core == 0, halves[:, :, :, 0], halves[:, :, :, 1]).reshape(chips, rows, cols)
    give_half = jnp.where(core == 0, halves[:, :, :, 1], halves[:, :, :, 0]).reshape(chips, rows, cols)
    got_half = other_core(give_half)
    first = jnp.where(core == 0, keep_half, got_half)
    second = jnp.where(core == 0, got_half, keep_half)
    ring = jnp.stack([first, second], axis=1)
    ring = jnp.concatenate([ring, ring], axis=0)
    full = lax.dynamic_slice_in_dim(ring, (chips - chip) % chips, chips, axis=0)
    full = full.reshape(chips * strip, cols)
    write_half, read_half = full[:, :half], full[:, half:]

    small = 4
    kq_rows = jnp.concatenate([key_rows[: tokens // small], query_rows[: asked_count // small]], axis=0)
    kq = by_features(kq_rows)
    key_strip = kq[:, :, :, : tokens // small].reshape(-1, strip)
    query_strip = kq[:, :, :, tokens // small :].reshape(-1, strip)

    hidden_pre = contract(write_half, key_pair, 0, 1)
    hidden = jax.nn.silu(hidden_pre).astype(wire)
    all_hidden = jnp.concatenate([hidden] + [from_chip(hidden, s) for s in range(1, chips)], axis=1)
    query_base = contract(write_half, query_pair, 0, 1)

    def over_hid(part):
        count = part.shape[0] // 2
        total = part[:count] + other_core(part[count:].astype(wire)).astype(jnp.float32)
        groups = total.reshape(4, count // 4, width)
        mine = groups[0]
        for k in range(1, 4):
            mine = mine + with_peer(groups[k].astype(wire), k).astype(jnp.float32)
        return mine

    output = over_hid(contract(hidden, read_half, 0, 1)).astype(wire)
    quarter = tokens // small
    delta_rows = row_scale[:quarter] * (
        key_rows[:quarter].astype(jnp.float32)
        + output.astype(jnp.float32)
        - value_rows[:quarter].astype(jnp.float32)
    )
    delta_strip = by_features(delta_rows.astype(wire)).reshape(-1, strip)
    output_rows = jnp.concatenate([output] + [with_peer(output, k) for k in range(1, 4)], axis=0)
    output_pair = jnp.concatenate([output_rows, other_core(output_rows)], axis=0)
    delta = scale_pair * (
        key_pair.astype(jnp.float32)
        + output_pair.astype(jnp.float32)
        - value_pair.astype(jnp.float32)
    )
    back = (contract(read_half, delta.astype(wire), 0, 1) * silu_slope(hidden_pre)).astype(wire)
    all_back = jnp.concatenate([back] + [from_chip(back, s) for s in range(1, chips)], axis=1)

    part_r = contract(all_hidden, delta_strip, 1, 0)
    part_w = contract(all_back, key_strip, 1, 0)

    norm = (jnp.sum(part_w * part_w) + jnp.sum(part_r * part_r)).reshape(1, 1)
    norm = jnp.broadcast_to(norm, (8, 128))
    norm = norm + other_core(norm)
    norm = norm + sum(with_peer(norm, k) for k in range(1, 4))
    norm = norm + sum(from_chip(norm, s) for s in range(1, chips))
    total = norm[0, 0]
    scale = jnp.minimum(1.0, radius / jnp.sqrt(total + 1e-06))
    keep = (1.0 - forget[0]) * (1.0 - forget[1])

    moved = contract(part_w.astype(wire), query_strip, 1, 1)
    span = 2 * asked_count
    query_move = moved[:, :span]
    for s in range(1, chips):
        query_move = query_move + to_chip(
            moved[:, span * s : span * (s + 1)].astype(wire), s
        ).astype(jnp.float32)
    query_hidden = jax.nn.silu(keep * query_base - scale * query_move).astype(wire)

    part_r_wire = part_r.astype(wire)
    strips = [part_r_wire] + [from_chip(part_r_wire, s) for s in range(1, chips)]
    turn = jnp.stack(strips + strips)
    turn = lax.dynamic_slice_in_dim(turn, (chips - chip) % chips, chips, axis=0)
    whole_r = jnp.concatenate([turn[j] for j in range(chips)], axis=1)
    answer = keep * contract(query_hidden, read_half, 0, 1) - scale * contract(
        query_hidden, whole_r, 0, 0
    )
    mine_rows = asked_count // 4
    recalled = (query_rows[:mine_rows].astype(jnp.float32) + over_hid(answer)).astype(wire)
    recalled = jnp.concatenate([recalled] + [with_peer(recalled, k) for k in range(1, 4)], axis=0)
    recalled = regroup(recalled, hid)

    parts = jnp.stack([part_w, part_r]).reshape(2, half, 2, rows)
    kept = jnp.where(core == 0, parts[:, :, 0], parts[:, :, 1])
    given = jnp.where(core == 0, parts[:, :, 1], parts[:, :, 0])
    got = other_core(given)
    low = jnp.where(core == 0, kept, got)
    high = jnp.where(core == 0, got, kept)
    own = jnp.concatenate([low, high], axis=1).transpose(0, 2, 1)
    new_write = keep * write_weight - scale * own[0]
    new_read = keep * read_weight - scale * own[1]
    return (new_write, new_read, recalled)


def times_transposed(left, right):
    return lax.dot_general(left, right, (((1,), (1,)), ((), ())), precision=highest)


def inner_rows(left, right):
    return lax.dot_general(left, right, (((0,), (0,)), ((), ())), precision=highest)


def many_devices(keys, values, queries, rates, forget, momentum, write_weight, read_weight):
    width = keys.shape[2]
    full_write, full_read = (
        lax.all_gather(write_weight, "tok", axis=0, tiled=True),
        lax.all_gather(read_weight, "tok", axis=0, tiled=True),
    )
    inputs = keys.reshape(-1, width).astype(jnp.float32)
    hidden_pre = jnp.dot(inputs, full_write, precision=highest)
    hidden = jax.nn.silu(hidden_pre)
    output = lax.psum(times_transposed(hidden, full_read).astype(jnp.bfloat16), "hid").astype(
        jnp.float32
    )
    error = inputs + output - values.reshape(-1, width).astype(jnp.float32)
    factor = 1.0 - forget[1] + momentum[0]
    per_block = jnp.stack([factor, jnp.ones_like(factor)])
    row_scale = (2.0 * rates * per_block[:, None]).reshape(-1, 1)
    delta = row_scale * error
    back = jnp.dot(delta, full_read, precision=highest) * silu_slope(hidden_pre)
    grad_write = inner_rows(inputs, back)
    grad_read = inner_rows(delta, hidden)
    part_w, part_r = (
        lax.psum_scatter(grad_write, "tok", scatter_dimension=0, tiled=True),
        lax.psum_scatter(grad_read, "tok", scatter_dimension=0, tiled=True),
    )
    keep = (1.0 - forget[0]) * (1.0 - forget[1])
    whole_w, whole_r = (
        lax.all_gather(part_w, "tok", axis=0, tiled=True),
        lax.all_gather(part_r, "tok", axis=0, tiled=True),
    )
    total = lax.psum(jnp.sum(whole_w * whole_w) + jnp.sum(whole_r * whole_r), "hid")
    scale = jnp.minimum(1.0, radius / jnp.sqrt(total + 1e-06))
    new_write = keep * write_weight - scale * part_w
    new_read = keep * read_weight - scale * part_r
    wide_write = keep * full_write - scale * whole_w
    wide_read = keep * full_read - scale * whole_r
    asked = queries.astype(jnp.float32)
    query_hidden = jax.nn.silu(jnp.dot(asked, wide_write, precision=highest))
    answer = lax.psum(times_transposed(query_hidden, wide_read), "hid")
    recalled = (asked + answer).astype(jnp.bfloat16)
    return (new_write, new_read, recalled)


def solution(mesh):
    in_specs = (
        P(None, "tok", None),
        P(None, "tok", None),
        P("tok", None),
        P(None, "tok"),
        P(),
        P(),
        P("tok", "hid"),
        P("tok", "hid"),
    )
    out_specs = (P("tok", "hid"), P("tok", "hid"), P("tok", None))
    paired = mesh.shape["hid"] == 4 and mesh.shape["tok"] == 8
    body = few_devices if paired else many_devices
    return jax.shard_map(
        body, mesh=mesh, in_specs=in_specs, out_specs=out_specs, check_vma=False
    )
```
